32 devices in a mesh: groups: 2 (over x), gx: 16 (over z, y, core).
Axes of the slice: x: 2, y: 2, z: 4, core: 2. Of those that a mesh axis runs over, the one named last changes fastest.
Arguments:
- volume: bfloat16 [32, 256, 6, 128], P('groups', 'gx'), parts along dimension 0, may hold values from -6 to 6
- conv_weight: bfloat16 [256, 27, 128], P('gx'), may hold values from -0.078125 to 0.078125
- conv_bias: float32 [128], replicated, may hold values from -3 to 3
- tconv_weight: bfloat16 [27, 64, 128], replicated, may hold values from -0.25 to 0.25
Outputs:
- decoded: bfloat16 [64, 64, 12, 256], P(('groups', 'gx')), parts along dimension 0
The draws below stay inside these ranges and needn't reach their ends.
There are 2 independent parts, one for each index of `groups`. The reference program is written for one: setup_inputs(seed, part) draws one part's arguments, and reference() takes and returns one part's arrays. A program takes and returns all parts, laid end to end along the dimension named above; an argument that names none is the same for every part. Nothing has to cross between parts.
All inputs are finite; a program needn't handle non-finite values.
Results may differ from the reference program's by a relative error of at most 0.005.
Values may be sent and summed in bfloat16 or wider, within the bound.
A program may use at most 64 MiB of HBM per device.

```python
import jax
import jax.numpy as jnp
from jax import lax

CIN = 256
COUT = 128
CUP = 64
WY = 6
WZ = 128
NX = 16


def raised(values, stream_key, source, target, blocks, factor):
    def block_of(axis_at):
        return (jnp.arange(values.shape[axis_at]) // (values.shape[axis_at] // blocks)).reshape((-1,) + (1,) * (values.ndim - 1 - axis_at))

    one_side = jax.random.permutation(stream_key, blocks)[block_of(target)]
    second = (block_of(target) + blocks // 2) % blocks
    return jnp.where((block_of(source) == one_side) | (block_of(source) == second), factor * values, values)


def block_scale(key, shape, shards, smallest, top_value):
    loudness = 1.0
    for axis_at, shards_of in shards:
        draws = jax.random.uniform(jax.random.fold_in(jax.random.fold_in(key, 6), axis_at), (shards_of,), jnp.float32, smallest / len(shards), top_value / len(shards))
        loudness = loudness * jnp.repeat(jnp.exp(draws), shape[axis_at] // shards_of).reshape((-1,) + (1,) * (len(shape) - 1 - axis_at))
    return loudness


def bell_draw(own_key, extent, width, reach, cuts=(), kind=jnp.bfloat16):
    factor_of = block_scale(own_key, extent, cuts, -0.22, 0.18) if cuts else 1.0
    values = jax.random.normal(own_key, extent, jnp.float32) * width * factor_of
    return jnp.minimum(jnp.maximum(values, -reach), reach).astype(kind)


def bell_draw_with(rng, dims, deviation, reach, shards, heavy, kind=jnp.bfloat16):
    entries = deviation * jax.random.normal(rng, dims, jnp.float32)
    if shards:
        entries = entries * block_scale(rng, dims, shards, -0.22, 0.18)
    return jnp.clip(raised(entries, jax.random.fold_in(rng, 3), *heavy), -reach, reach).astype(kind)


def setup_inputs(seed: int = 0, part: int = 0) -> dict:
    arg_keys = jax.random.split(jax.random.key(seed), 5)
    part_splits = jax.random.split(jax.random.fold_in(arg_keys[4], part), 5)
    volume = bell_draw_with(part_splits[0], (NX, CIN, WY, WZ), 1.0, 6.0, ((1, 16),), (1, 0, 16, 2.0))
    conv_weight = bell_draw(arg_keys[1], (CIN, 27, COUT), (CIN * 27) ** -0.5, 0.078125, ((0, 16),))
    conv_bias = bell_draw(arg_keys[2], (COUT,), 0.5, 3.0, (), jnp.float32)
    tconv_weight = bell_draw(arg_keys[3], (27, CUP, COUT), (COUT * 4) ** -0.5, 0.25)
    return {"volume": volume, "conv_weight": conv_weight, "conv_bias": conv_bias, "tconv_weight": tconv_weight}


def next_cell(field, axis):
    size = field.shape[axis]
    rest = lax.slice_in_dim(field, 1, size, axis=axis)
    zero_shape = list(field.shape)
    zero_shape[axis] = 1
    return jnp.concatenate([rest, jnp.zeros(zero_shape, field.dtype)], axis=axis)


def yz_classes(products, tap_x):
    layout_options = (((1, False),), ((2, False), (0, True)))
    parity_classes = []
    for par_y in range(2):
        for par_z in range(2):
            total = jnp.zeros(products.shape[:1] + products.shape[4:], jnp.float32)
            for tap_y, shift_y in layout_options[par_y]:
                for tap_z, shift_z in layout_options[par_z]:
                    term = products[:, tap_x, tap_y, tap_z]
                    if shift_y:
                        term = next_cell(term, 2)
                    if shift_z:
                        term = next_cell(term, 3)
                    total = total + term
            parity_classes.append(total)
    return jnp.stack(parity_classes, axis=0)


def alternate(even, odd):
    both = jnp.stack([even, odd], axis=0)
    rows, chans, wide_y, wide_z = both.shape[2], both.shape[3], both.shape[4], both.shape[5]
    both = both.reshape(2, 2, 2, rows, chans, wide_y, wide_z)
    both = jnp.transpose(both, (3, 0, 4, 5, 1, 6, 2))
    return both.reshape(2 * rows, chans, 2 * wide_y, 2 * wide_z)


def reference(volume, conv_weight, conv_bias, tconv_weight):
    cin, cout = conv_weight.shape[0], conv_weight.shape[2]
    kernel = conv_weight.reshape(cin, 3, 3, 3, cout)
    kernel = jnp.transpose(kernel, (4, 0, 1, 2, 3))
    lhs = jnp.transpose(volume, (1, 0, 2, 3))[None]
    conv = lax.conv_general_dilated(lhs, kernel, (1, 1, 1), [(1, 1), (1, 1), (1, 1)],
                                    dimension_numbers=("NCDHW", "OIDHW", "NCDHW"),
                                    preferred_element_type=jnp.float32)
    conv = jnp.transpose(conv[0], (1, 0, 2, 3))
    hidden = jnp.maximum(conv + conv_bias[None, :, None, None], 0.0).astype(jnp.bfloat16)
    cup = tconv_weight.shape[1]
    rows, wide_y, wide_z = hidden.shape[0], hidden.shape[2], hidden.shape[3]
    flattened_patches = tconv_weight.reshape(27 * cup, cout).astype(jnp.float32)
    products = jnp.einsum("oc,xcyz->xoyz", flattened_patches, hidden.astype(jnp.float32))
    products = products.reshape(rows, 3, 3, 3, cup, wide_y, wide_z)
    first = yz_classes(products, 0)
    middle = yz_classes(products, 1)
    last = yz_classes(products, 2)
    odd = last + next_cell(first, 1)
    return alternate(middle, odd).astype(jnp.bfloat16)
```

```python
import jax
import jax.numpy as jnp
from jax import lax
from jax.experimental import pallas as pl
from jax.experimental.pallas import tpu as pltpu
from jax.sharding import PartitionSpec as P

MESH = pl.DeviceIdType.MESH
VMEM = pl.BlockSpec(memory_space=pltpu.VMEM)
ANY = pl.BlockSpec(memory_space=pl.ANY)


def shift_up(block):
    lane = lax.broadcasted_iota(jnp.int32, block.shape, 1)
    return jnp.where(lane == 0, 0.0, pltpu.roll(block, 1, axis=1))


def shift_down(block):
    size = block.shape[1]
    lane = lax.broadcasted_iota(jnp.int32, block.shape, 1)
    return jnp.where(lane == size - 1, 0.0, pltpu.roll(block, size - 1, axis=1))


def conv_hidden(planes, wide_y, wide_z, tap, bias):
    zero = jnp.zeros_like(planes[0](0))
    total = None
    for kx in range(3):
        padded = jnp.concatenate(
            [zero] + [planes[kx](y) for y in range(wide_y)] + [zero], axis=1
        )
        for ky in range(3):
            weight = jnp.concatenate([tap(kx * 9 + ky * 3 + kz) for kz in range(3)], axis=1)
            cells = padded[:, ky * wide_z : (ky + wide_y) * wide_z]
            term = lax.dot_general(
                weight, cells, (((0,), (0,)), ((), ())), preferred_element_type=jnp.float32
            )
            total = term if total is None else total + term
    cout = total.shape[0] // 3
    rows = []
    for y in range(wide_y):
        part = total[:, y * wide_z : (y + 1) * wide_z]
        rows.append(
            part[cout : 2 * cout]
            + shift_up(part[:cout])
            + shift_down(part[2 * cout :])
        )
    summed = jnp.concatenate(rows, axis=1)
    return jnp.maximum(summed + bias, 0.0).astype(jnp.bfloat16)


def exchange_conv(volume, weight, bias, hidden_out, planes, weights, hidden, entry_sem,
                  vsend, vrecv, hsend, hrecv, wsend, wrecv, xsend, csend, crecv, esend, erecv):
    me = lax.axis_index("gx")
    count = lax.axis_size("gx")
    group = lax.axis_index("groups")
    chips = count // 2
    chip, core = me // 2, me % 2
    wide_y, wide_z = volume.shape[1], volume.shape[3]

    barrier = pltpu.get_barrier_semaphore()
    for d in range(1, count):
        pl.semaphore_signal(
            barrier, inc=1, device_id={"gx": (me + d) % count}, device_id_type=MESH
        )
    pl.semaphore_signal(barrier, inc=1, device_id={"groups": 1 - group}, device_id_type=MESH)
    pl.semaphore_wait(barrier, count)

    def remote(src, dst, send, recv, target):
        return pltpu.make_async_remote_copy(
            src_ref=src, dst_ref=dst, send_sem=send, recv_sem=recv,
            device_id=target, device_id_type=MESH,
        )

    own_volume = pltpu.make_async_copy(volume.at[me], planes.at[1, me], entry_sem.at[0])
    own_weight = pltpu.make_async_copy(weight, weights.at[me], entry_sem.at[1])
    own_volume.start()
    own_weight.start()

    def piece(d):
        to = (me + d) % count
        return remote(volume.at[to], planes.at[1, me], vsend.at[d], vrecv.at[d], {"gx": to})

    order = [d for pair in zip(range(1, count // 2), range(count - 1, count // 2, -1)) for d in pair]
    order.append(count // 2)
    for d in order:
        piece(d).start()

    def source(k):
        return (chip + chips - k) % chips

    def leads(c):
        return (c // 2 + c) % 2 == group

    def direct(k):
        to = ((chip + k) % chips) * 2 + core
        return remote(weight, weights.at[me], wsend.at[k], wrecv.at[k], {"gx": to})

    def across(k):
        at = weights.at[source(k) * 2 + core]
        return remote(at, at, xsend.at[k], wrecv.at[k], {"groups": 1 - group})

    def beside(k):
        slot = source(k) * 2 + core
        src = weight if k == 0 else weights.at[slot]
        return remote(src, weights.at[slot], csend.at[k], crecv.at[k], {"gx": chip * 2 + 1 - core})

    def beside_arrival(k):
        slot = source(k) * 2 + 1 - core
        at = weights.at[slot]
        return remote(at, at, csend.at[k], crecv.at[k], {"gx": chip * 2 + 1 - core})

    beside(0).start()

    @pl.when(leads(chip))
    def _():
        for k in range(1, chips):
            direct(k).start()

    @pl.when(me == 0)
    def _():
        planes[0] = jnp.zeros(planes.shape[1:], planes.dtype)

    @pl.when(me == count - 1)
    def _():
        planes[2] = jnp.zeros(planes.shape[1:], planes.dtype)
        hidden[1] = jnp.zeros(hidden.shape[1:], hidden.dtype)

    def arrived(at, sem):
        pltpu.make_async_copy(at, at, sem).wait()

    own_volume.wait()
    for d in order:
        arrived(planes.at[1, (me + count - d) % count], vrecv.at[d])

    def to_right():
        return remote(planes.at[1], planes.at[0], hsend.at[0], hrecv.at[0], {"gx": me + 1})

    def to_left():
        return remote(planes.at[1], planes.at[2], hsend.at[1], hrecv.at[1], {"gx": me - 1})

    @pl.when(me < count - 1)
    def _():
        to_right().start()

    @pl.when(me > 0)
    def _():
        to_left().start()

    for wanted in (True, False):
        for k in range(1, chips):
            @pl.when(leads(source(k)) == wanted)
            def _(k=k, wanted=wanted):
                arrived(weights.at[source(k) * 2 + core], wrecv.at[k])
                if wanted:
                    across(k).start()
                beside(k).start()

    own_weight.wait()
    for k in range(chips):
        arrived(weights.at[source(k) * 2 + 1 - core], crecv.at[k])

    @pl.when(me > 0)
    def _():
        arrived(planes.at[0], hrecv.at[0])

    @pl.when(me < count - 1)
    def _():
        arrived(planes.at[2], hrecv.at[1])

    cin = count * volume.shape[2]
    cells = [lambda y, kx=kx: planes[kx, :, y].reshape(cin, wide_z) for kx in range(3)]
    hidden[0] = conv_hidden(
        cells, wide_y, wide_z, lambda t: weights[:, t].reshape(cin, weights.shape[3]), bias[...]
    )

    def edge():
        return remote(hidden.at[0], hidden.at[1], esend, erecv, {"gx": me - 1})

    @pl.when(me > 0)
    def _():
        edge().start()

    for d in order:
        piece(d).wait_send()

    @pl.when(leads(chip))
    def _():
        for k in range(1, chips):
            direct(k).wait_send()

    for k in range(1, chips):
        @pl.when(leads(source(k)))
        def _(k=k):
            across(k).wait_send()

    for k in range(chips):
        beside(k).wait_send()

    @pl.when(me < count - 1)
    def _():
        to_right().wait_send()

    @pl.when(me > 0)
    def _():
        to_left().wait_send()

    @pl.when(me < count - 1)
    def _():
        arrived(hidden.at[1], erecv)

    @pl.when(me > 0)
    def _():
        edge().wait_send()

    hidden_out[...] = hidden[...]


def local_conv(planes, weight, bias, hidden_out):
    wide_y, wide_z = planes.shape[1], planes.shape[3]
    cells = [lambda y, kx=kx: planes[kx, y] for kx in range(3)]
    hidden_out[...] = conv_hidden(cells, wide_y, wide_z, lambda t: weight[t], bias[...])


def transposed(hidden, tconv, out):
    wide_z = out.shape[3] // 2
    wide_y = out.shape[1] // 2
    cup = tconv.shape[1]
    cout = tconv.shape[2]
    here, after = hidden[0], hidden[1]

    def down(x):
        return jnp.concatenate([x[:, wide_z:], jnp.zeros_like(x[:, :wide_z])], axis=1)

    def taps(kx, ky):
        t = kx * 9 + ky * 3
        return tconv[t : t + 3].reshape(3 * cup, cout)

    row = lax.broadcasted_iota(jnp.int32, (2 * wide_z, 2 * wide_z), 0)
    col = lax.broadcasted_iota(jnp.int32, (2 * wide_z, 2 * wide_z), 1)
    spread = jnp.where(
        col == jnp.where(row < wide_z, 2 * row, 2 * (row - wide_z) + 1), 1.0, 0.0
    ).astype(jnp.bfloat16)
    x_options = (((1, here),), ((2, here), (0, after)))
    for pu in range(2):
        for pv in range(2):
            left, right = [], []
            for kx, field in x_options[pu]:
                for ky, shifted in (((1, False),), ((2, False), (0, True)))[pv]:
                    left.append(taps(kx, ky))
                    right.append(down(field) if shifted else field)
            product = jnp.dot(
                jnp.concatenate(left, axis=1), jnp.concatenate(right, axis=0),
                preferred_element_type=jnp.float32,
            )
            pairs = []
            for y in range(wide_y):
                part = product[:, y * wide_z : (y + 1) * wide_z]
                even = part[cup : 2 * cup]
                odd = part[2 * cup :] + shift_down(part[:cup])
                pairs.append(jnp.concatenate([even, odd], axis=1).astype(jnp.bfloat16))
            mixed = jnp.dot(
                jnp.concatenate(pairs, axis=0), spread, preferred_element_type=jnp.float32
            ).astype(jnp.bfloat16)
            for y in range(wide_y):
                out[pu, 2 * y + pv] = mixed[y * cup : (y + 1) * cup]


def native_hidden(volume, conv_weight, bias):
    count = lax.axis_size("gx")
    forward = [(i, i + 1) for i in range(count - 1)]
    backward = [(i + 1, i) for i in range(count - 1)]
    local = lax.all_to_all(volume, "gx", split_axis=0, concat_axis=1, tiled=True)
    weight = lax.all_gather(conv_weight, "gx", axis=0, tiled=True)
    rows = local.shape[0]
    low = lax.ppermute(local[rows - 1 :], "gx", forward)
    high = lax.ppermute(local[:1], "gx", backward)
    planes = jnp.transpose(jnp.concatenate([low, local, high], axis=0), (0, 2, 1, 3))
    weight = jnp.transpose(weight, (1, 0, 2))
    cout = weight.shape[2]
    shape = jax.ShapeDtypeStruct((cout, planes.shape[1] * planes.shape[3]), jnp.bfloat16)
    conv = pl.pallas_call(
        local_conv, out_shape=shape, in_specs=[VMEM] * 3, out_specs=VMEM,
        compiler_params=pltpu.CompilerParams(vmem_limit_bytes=40 << 20),
    )
    hidden = [conv(planes[r : r + 3], weight, bias) for r in range(rows)]
    hidden.append(lax.ppermute(hidden[0], "gx", backward))
    return [jnp.stack(hidden[r : r + 2]) for r in range(rows)]


def remote_hidden(volume, conv_weight, bias):
    count = lax.axis_size("gx")
    chips = count // 2
    cells = jnp.transpose(volume, (0, 2, 1, 3))
    weight = jnp.transpose(conv_weight, (1, 0, 2))
    cout = weight.shape[2]
    lanes = cells.shape[1] * cells.shape[3]
    dma = pltpu.SemaphoreType.DMA
    hidden = pl.pallas_call(
        exchange_conv,
        out_shape=jax.ShapeDtypeStruct((2, cout, lanes), jnp.bfloat16),
        in_specs=[ANY, ANY, VMEM],
        out_specs=VMEM,
        scratch_shapes=[
            pltpu.VMEM((3, count) + cells.shape[1:], jnp.bfloat16),
            pltpu.VMEM((count,) + weight.shape, jnp.bfloat16),
            pltpu.VMEM((2, cout, lanes), jnp.bfloat16),
            dma((2,)),
            dma((count,)), dma((count,)),
            dma((2,)), dma((2,)),
            dma((chips,)), dma((chips,)), dma((chips,)),
            dma((chips,)), dma((chips,)),
            dma(()), dma(()),
        ],
        compiler_params=pltpu.CompilerParams(
            collective_id=0, has_side_effects=True, vmem_limit_bytes=40 << 20
        ),
    )(cells, weight, bias)
    return [hidden]


def per_device(volume, conv_weight, conv_bias, tconv_weight):
    count = lax.axis_size("gx")
    rows = volume.shape[0] // count
    bias = conv_bias[:, None]
    suited = (
        rows == 1 and count == 16 and lax.axis_size("groups") == 2
        and volume.shape[1] % 16 == 0
    )
    hidden = (remote_hidden if suited else native_hidden)(volume, conv_weight, bias)
    cup = tconv_weight.shape[1]
    shape = jax.ShapeDtypeStruct(
        (2, 2 * volume.shape[2], cup, 2 * volume.shape[3]), jnp.bfloat16
    )
    tconv = pl.pallas_call(
        transposed, out_shape=shape, in_specs=[VMEM] * 2, out_specs=VMEM,
        compiler_params=pltpu.CompilerParams(vmem_limit_bytes=40 << 20),
    )
    outs = [tconv(planes, tconv_weight) for planes in hidden]
    out = outs[0] if len(outs) == 1 else jnp.concatenate(outs, axis=0)
    return jnp.transpose(out, (0, 2, 1, 3))


def solution(mesh):
    return jax.shard_map(
        per_device,
        mesh=mesh,
        in_specs=(P("groups", "gx", None, None), P("gx", None, None), P(), P()),
        out_specs=P(("groups", "gx"), None, None, None),
        check_vma=False,
    )
```

```python
import jax
import jax.numpy as jnp
from jax import lax
from jax.experimental import pallas as pl
from jax.experimental.pallas import tpu as pltpu
from jax.sharding import PartitionSpec as P

MESH = pl.DeviceIdType.MESH
VMEM = pl.BlockSpec(memory_space=pltpu.VMEM)
HBM = pl.BlockSpec(memory_space=pltpu.HBM)


def shift_up(block):
    lane = lax.broadcasted_iota(jnp.int32, block.shape, 1)
    return jnp.where(lane == 0, 0.0, pltpu.roll(block, 1, axis=1))


def shift_down(block):
    size = block.shape[1]
    lane = lax.broadcasted_iota(jnp.int32, block.shape, 1)
    return jnp.where(lane == size - 1, 0.0, pltpu.roll(block, size - 1, axis=1))


def conv_hidden(planes, wide_y, wide_z, tap, bias):
    zero = jnp.zeros_like(planes[0](0))
    total = None
    for kx in range(3):
        padded = jnp.concatenate(
            [zero] + [planes[kx](y) for y in range(wide_y)] + [zero], axis=1
        )
        for ky in range(3):
            weight = jnp.concatenate([tap(kx * 9 + ky * 3 + kz) for kz in range(3)], axis=1)
            cells = padded[:, ky * wide_z : (ky + wide_y) * wide_z]
            term = lax.dot_general(
                weight, cells, (((0,), (0,)), ((), ())), preferred_element_type=jnp.float32
            )
            total = term if total is None else total + term
    cout = total.shape[0] // 3
    rows = []
    for y in range(wide_y):
        part = total[:, y * wide_z : (y + 1) * wide_z]
        rows.append(
            part[cout : 2 * cout]
            + shift_up(part[:cout])
            + shift_down(part[2 * cout :])
            + bias
        )
    return jnp.maximum(jnp.concatenate(rows, axis=1), 0.0).astype(jnp.bfloat16)


def exchange_conv(volume, weight, bias, hidden_out, planes, weights, hidden, bias_row, entry_sem,
                  vsend, vrecv, hsend, hrecv, wsend, rsend, wrecv, xsend, csend, crecv, esend, erecv):
    me = lax.axis_index("gx")
    count = lax.axis_size("gx")
    group = lax.axis_index("groups")
    chips = count // 2
    chip, core = me // 2, me % 2
    wide_y, wide_z = volume.shape[1], volume.shape[3]

    barrier = pltpu.get_barrier_semaphore()
    for d in range(1, count):
        pl.semaphore_signal(
            barrier, inc=1, device_id={"gx": (me + d) % count}, device_id_type=MESH
        )
    pl.semaphore_signal(barrier, inc=1, device_id={"groups": 1 - group}, device_id_type=MESH)
    pl.semaphore_wait(barrier, count)

    def remote(src, dst, send, recv, target):
        return pltpu.make_async_remote_copy(
            src_ref=src, dst_ref=dst, send_sem=send, recv_sem=recv,
            device_id=target, device_id_type=MESH,
        )

    own_volume = pltpu.make_async_copy(volume.at[me], planes.at[1, me], entry_sem.at[0])
    own_weight = pltpu.make_async_copy(weight, weights.at[me], entry_sem.at[1])
    own_bias = pltpu.make_async_copy(bias, bias_row, entry_sem.at[2])

    half = chips // 2
    place = chip % half
    base = chip - place
    mirror = (chip + half) % chips

    def near(j):
        return base + (place + j) % half

    def far(j):
        return (half - base) + (place + j) % half

    def leads(c):
        return (c // 2 + c) % 2 == group

    def direct(j):
        to = mirror if j == 0 else near(j)
        return remote(weight, weights.at[me], wsend.at[j], wrecv.at[chip], {"gx": to * 2 + core})

    def relay(j):
        at = weights.at[mirror * 2 + core]
        return remote(at, at, rsend.at[j], wrecv.at[mirror], {"gx": near(j) * 2 + core})

    def across(c):
        at = weights.at[c * 2 + core]
        return remote(at, at, xsend.at[c], wrecv.at[c], {"groups": 1 - group})

    def beside(c, own=False):
        slot = c * 2 + core
        src = weight if own else weights.at[slot]
        return remote(src, weights.at[slot], csend.at[c], crecv.at[c], {"gx": chip * 2 + 1 - core})

    def piece(d):
        to = (me + d) % count
        return remote(volume.at[to], planes.at[1, me], vsend.at[d], vrecv.at[d], {"gx": to})

    def arrived(at, sem):
        pltpu.make_async_copy(at, at, sem).wait()

    order = [d for pair in zip(range(1, count // 2), range(count - 1, count // 2, -1)) for d in pair]
    order = [count // 2] + order[::-1]
    others = [mirror] + [near(j) for j in range(1, half)] + [far(j) for j in range(1, half)]

    @pl.when(leads(chip))
    def _():
        for j in range(half):
            direct(j).start()

    for d in order:
        piece(d).start()
    beside(chip, True).start()
    own_volume.start()
    own_weight.start()
    own_bias.start()

    @pl.when(me == 0)
    def _():
        planes[0] = jnp.zeros(planes.shape[1:], planes.dtype)

    @pl.when(me == count - 1)
    def _():
        planes[2] = jnp.zeros(planes.shape[1:], planes.dtype)
        hidden[1] = jnp.zeros(hidden.shape[1:], hidden.dtype)

    for c in others:
        @pl.when(leads(c))
        def _(c=c):
            arrived(weights.at[c * 2 + core], wrecv.at[c])
            if c is mirror:
                for j in range(1, half):
                    relay(j).start()
            across(c).start()
            beside(c).start()

    own_volume.wait()
    for d in order:
        arrived(planes.at[1, (me + count - d) % count], vrecv.at[d])

    def to_right():
        return remote(planes.at[1], planes.at[0], hsend.at[0], hrecv.at[0], {"gx": me + 1})

    def to_left():
        return remote(planes.at[1], planes.at[2], hsend.at[1], hrecv.at[1], {"gx": me - 1})

    @pl.when(me < count - 1)
    def _():
        to_right().start()

    @pl.when(me > 0)
    def _():
        to_left().start()

    for c in others:
        @pl.when(jnp.logical_not(leads(c)))
        def _(c=c):
            arrived(weights.at[c * 2 + core], wrecv.at[c])
            beside(c).start()

    own_weight.wait()
    own_bias.wait()
    for c in [chip] + others:
        arrived(weights.at[c * 2 + 1 - core], crecv.at[c])

    @pl.when(me > 0)
    def _():
        arrived(planes.at[0], hrecv.at[0])

    @pl.when(me < count - 1)
    def _():
        arrived(planes.at[2], hrecv.at[1])

    cin = count * volume.shape[2]
    cells = [lambda y, kx=kx: planes[kx, :, y].reshape(cin, wide_z) for kx in range(3)]
    hidden[0] = conv_hidden(
        cells, wide_y, wide_z, lambda t: weights[:, t].reshape(cin, weights.shape[3]),
        jnp.transpose(jnp.broadcast_to(bias_row[...], (wide_z, bias_row.shape[1]))),
    )

    def edge():
        return remote(hidden.at[0], hidden.at[1], esend, erecv, {"gx": me - 1})

    @pl.when(me > 0)
    def _():
        edge().start()

    for d in order:
        piece(d).wait_send()

    @pl.when(leads(chip))
    def _():
        for j in range(half):
            direct(j).wait_send()
        for j in range(1, half):
            relay(j).wait_send()

    beside(chip, True).wait_send()
    for c in others:
        @pl.when(leads(c))
        def _(c=c):
            across(c).wait_send()

        beside(c).wait_send()

    @pl.when(me < count - 1)
    def _():
        to_right().wait_send()

    @pl.when(me > 0)
    def _():
        to_left().wait_send()

    @pl.when(me < count - 1)
    def _():
        arrived(hidden.at[1], erecv)

    @pl.when(me > 0)
    def _():
        edge().wait_send()

    hidden_out[...] = hidden[...]


def local_conv(planes, weight, bias, hidden_out):
    wide_y, wide_z = planes.shape[1], planes.shape[3]
    cells = [lambda y, kx=kx: planes[kx, y] for kx in range(3)]
    hidden_out[...] = conv_hidden(cells, wide_y, wide_z, lambda t: weight[t], bias[...])


def transposed(hidden, tconv, out):
    wide_z = out.shape[3] // 2
    wide_y = out.shape[1] // 2
    cup = tconv.shape[1]
    cout = tconv.shape[2]
    here, after = hidden[0], hidden[1]

    def down(x):
        return jnp.concatenate([x[:, wide_z:], jnp.zeros_like(x[:, :wide_z])], axis=1)

    def taps(kx, ky):
        t = kx * 9 + ky * 3
        return tconv[t : t + 3].reshape(3 * cup, cout)

    row = lax.broadcasted_iota(jnp.int32, (2 * wide_z, 2 * wide_z), 0)
    col = lax.broadcasted_iota(jnp.int32, (2 * wide_z, 2 * wide_z), 1)
    spread = jnp.where(
        col == jnp.where(row < wide_z, 2 * row, 2 * (row - wide_z) + 1), 1.0, 0.0
    ).astype(jnp.bfloat16)
    x_options = (((1, here),), ((2, here), (0, after)))
    for pu in range(2):
        for pv in range(2):
            left, right = [], []
            for kx, field in x_options[pu]:
                for ky, shifted in (((1, False),), ((2, False), (0, True)))[pv]:
                    left.append(taps(kx, ky))
                    right.append(down(field) if shifted else field)
            product = jnp.dot(
                jnp.concatenate(left, axis=1), jnp.concatenate(right, axis=0),
                preferred_element_type=jnp.float32,
            )
            pairs = []
            for y in range(wide_y):
                part = product[:, y * wide_z : (y + 1) * wide_z]
                even = part[cup : 2 * cup]
                odd = part[2 * cup :] + shift_down(part[:cup])
                pairs.append(jnp.concatenate([even, odd], axis=1).astype(jnp.bfloat16))
            mixed = jnp.dot(
                jnp.concatenate(pairs, axis=0), spread, preferred_element_type=jnp.float32
            ).astype(jnp.bfloat16)
            for y in range(wide_y):
                out[pu, 2 * y + pv] = mixed[y * cup : (y + 1) * cup]


def native_hidden(volume, conv_weight, bias):
    count = lax.axis_size("gx")
    forward = [(i, i + 1) for i in range(count - 1)]
    backward = [(i + 1, i) for i in range(count - 1)]
    local = lax.all_to_all(volume, "gx", split_axis=0, concat_axis=1, tiled=True)
    weight = lax.all_gather(conv_weight, "gx", axis=0, tiled=True)
    rows = local.shape[0]
    low = lax.ppermute(local[rows - 1 :], "gx", forward)
    high = lax.ppermute(local[:1], "gx", backward)
    planes = jnp.transpose(jnp.concatenate([low, local, high], axis=0), (0, 2, 1, 3))
    weight = jnp.transpose(weight, (1, 0, 2))
    cout = weight.shape[2]
    shape = jax.ShapeDtypeStruct((cout, planes.shape[1] * planes.shape[3]), jnp.bfloat16)
    conv = pl.pallas_call(
        local_conv, out_shape=shape, in_specs=[VMEM] * 3, out_specs=VMEM,
        compiler_params=pltpu.CompilerParams(vmem_limit_bytes=40 << 20),
    )
    hidden = [conv(planes[r : r + 3], weight, bias) for r in range(rows)]
    hidden.append(lax.ppermute(hidden[0], "gx", backward))
    return [jnp.stack(hidden[r : r + 2]) for r in range(rows)]


def remote_hidden(volume, conv_weight, bias):
    count = lax.axis_size("gx")
    chips = count // 2
    cells = jnp.transpose(volume, (0, 2, 1, 3))
    weight = jnp.transpose(conv_weight, (1, 0, 2))
    cout = weight.shape[2]
    lanes = cells.shape[1] * cells.shape[3]
    dma = pltpu.SemaphoreType.DMA
    hidden = pl.pallas_call(
        exchange_conv,
        out_shape=jax.ShapeDtypeStruct((2, cout, lanes), jnp.bfloat16),
        in_specs=[HBM, HBM, HBM],
        out_specs=VMEM,
        scratch_shapes=[
            pltpu.VMEM((3, count) + cells.shape[1:], jnp.bfloat16),
            pltpu.VMEM((count,) + weight.shape, jnp.bfloat16),
            pltpu.VMEM((2, cout, lanes), jnp.bfloat16),
            pltpu.VMEM((1, cout), jnp.float32),
            dma((3,)),
            dma((count,)), dma((count,)),
            dma((2,)), dma((2,)),
            dma((chips,)), dma((chips,)), dma((chips,)),
            dma((chips,)), dma((chips,)), dma((chips,)),
            dma(()), dma(()),
        ],
        compiler_params=pltpu.CompilerParams(
            collective_id=0, has_side_effects=True, vmem_limit_bytes=40 << 20
        ),
    )(cells, weight, bias.reshape(1, cout))
    return [hidden]


def per_device(volume, conv_weight, conv_bias, tconv_weight):
    count = lax.axis_size("gx")
    rows = volume.shape[0] // count
    bias = conv_bias[:, None]
    suited = (
        rows == 1 and count == 16 and lax.axis_size("groups") == 2
        and volume.shape[1] % 16 == 0
    )
    hidden = (remote_hidden if suited else native_hidden)(volume, conv_weight, bias)
    cup = tconv_weight.shape[1]
    shape = jax.ShapeDtypeStruct(
        (2, 2 * volume.shape[2], cup, 2 * volume.shape[3]), jnp.bfloat16
    )
    tconv = pl.pallas_call(
        transposed, out_shape=shape, in_specs=[VMEM] * 2, out_specs=VMEM,
        compiler_params=pltpu.CompilerParams(vmem_limit_bytes=40 << 20),
    )
    outs = [tconv(planes, tconv_weight) for planes in hidden]
    out = outs[0] if len(outs) == 1 else jnp.concatenate(outs, axis=0)
    return jnp.transpose(out, (0, 2, 1, 3))


def solution(mesh):
    return jax.shard_map(
        per_device,
        mesh=mesh,
        in_specs=(P("groups", "gx", None, None), P("gx", None, None), P(), P()),
        out_specs=P(("groups", "gx"), None, None, None),
        check_vma=False,
    )
```

```python
import jax
import jax.numpy as jnp
from jax import lax
from jax.experimental import pallas as pl
from jax.experimental.pallas import tpu as pltpu
from jax.sharding import PartitionSpec as P

MESH = pl.DeviceIdType.MESH
VMEM = pl.BlockSpec(memory_space=pltpu.VMEM)
HBM = pl.BlockSpec(memory_space=pltpu.HBM)


def shift_up(block):
    lane = lax.broadcasted_iota(jnp.int32, block.shape, 1)
    return jnp.where(lane == 0, 0.0, pltpu.roll(block, 1, axis=1))


def shift_down(block):
    size = block.shape[1]
    lane = lax.broadcasted_iota(jnp.int32, block.shape, 1)
    return jnp.where(lane == size - 1, 0.0, pltpu.roll(block, size - 1, axis=1))


def conv_hidden(planes, wide_y, wide_z, tap, bias):
    zero = jnp.zeros_like(planes[0](0))
    total = None
    for kx in range(3):
        padded = jnp.concatenate(
            [zero] + [planes[kx](y) for y in range(wide_y)] + [zero], axis=1
        )
        for ky in range(3):
            weight = jnp.concatenate([tap(kx * 9 + ky * 3 + kz) for kz in range(3)], axis=1)
            cells = padded[:, ky * wide_z : (ky + wide_y) * wide_z]
            term = lax.dot_general(
                weight, cells, (((0,), (0,)), ((), ())), preferred_element_type=jnp.float32
            )
            total = term if total is None else total + term
    cout = total.shape[0] // 3
    rows = []
    for y in range(wide_y):
        part = total[:, y * wide_z : (y + 1) * wide_z]
        rows.append(
            part[cout : 2 * cout]
            + shift_up(part[:cout])
            + shift_down(part[2 * cout :])
            + bias
        )
    return jnp.maximum(jnp.concatenate(rows, axis=1), 0.0).astype(jnp.bfloat16)


def exchange_conv(volume, weight, bias, hidden_out, planes, weights, hidden, bias_row, entry_sem,
                  vsend, vrecv, osend, orecv, hsend, hrecv, psend, precv,
                  wsend, rsend, wrecv, xsend, csend, crecv, esend, erecv):
    me = lax.axis_index("gx")
    count = lax.axis_size("gx")
    group = lax.axis_index("groups")
    chips = count // 2
    chip, core = me // 2, me % 2
    beds = count // 4
    bed, row = me // 4, chip % 2
    partner = me + 1 - 2 * core
    wide_y, wide_z = volume.shape[1], volume.shape[3]
    taps = weight.shape[0]
    cuts = ((0, (taps + 1) // 2), ((taps + 1) // 2, taps // 2))

    barrier = pltpu.get_barrier_semaphore()
    for d in range(1, count):
        pl.semaphore_signal(
            barrier, inc=1, device_id={"gx": (me + d) % count}, device_id_type=MESH
        )
    pl.semaphore_signal(barrier, inc=1, device_id={"groups": 1 - group}, device_id_type=MESH)
    pl.semaphore_wait(barrier, count)

    def remote(src, dst, send, recv, target):
        return pltpu.make_async_remote_copy(
            src_ref=src, dst_ref=dst, send_sem=send, recv_sem=recv,
            device_id=target, device_id_type=MESH,
        )

    def arrived(at, sem):
        pltpu.make_async_copy(at, at, sem).wait()

    inner = (me > 0) & (me < count - 1)
    outer = me - 1 + 2 * core
    own_volume = pltpu.make_async_copy(volume.at[me], planes.at[1, me], entry_sem.at[0])
    own_weight = pltpu.make_async_copy(weight, weights.at[me], entry_sem.at[1])
    own_bias = pltpu.make_async_copy(bias, bias_row, entry_sem.at[2])

    def own_outer():
        return pltpu.make_async_copy(
            volume.at[outer], planes.at[2 * core, me], entry_sem.at[3]
        )

    half = chips // 2
    place = chip % half
    base = chip - place
    mirror = (chip + half) % chips

    def near(j):
        return base + (place + j) % half

    def far(j):
        return (half - base) + (place + j) % half

    others = [mirror] + [near(j) for j in range(1, half)] + [far(j) for j in range(1, half)]

    def shard(slot, q):
        return weights.at[slot, pl.ds(*cuts[q])]

    def direct(q, j):
        to = mirror if j == 0 else near(j)
        return remote(
            weight.at[pl.ds(*cuts[q])], shard(me, q), wsend.at[j], wrecv.at[q, chip],
            {"gx": to * 2 + core},
        )

    def relay(q, j):
        at = shard(mirror * 2 + core, q)
        return remote(at, at, rsend.at[j], wrecv.at[q, mirror], {"gx": near(j) * 2 + core})

    def across(q, c):
        at = shard(c * 2 + core, q)
        return remote(at, at, xsend.at[c], wrecv.at[q, c], {"groups": 1 - group})

    def beside(q, c, own=False):
        at = shard(c * 2 + core, q)
        src = weight.at[pl.ds(*cuts[q])] if own else at
        return remote(src, at, csend.at[q, c], crecv.at[q, c], {"gx": partner})

    def piece(d):
        to = (me + d) % count
        return remote(volume.at[to], planes.at[1, me], vsend.at[d], vrecv.at[me], {"gx": to})

    def mates():
        found = [(0, partner, 1 - core)]
        for db in range(1, beds):
            for cc in range(2):
                found.append((2 * db + cc, ((bed + db) % beds) * 4 + row * 2 + cc, cc))
        return found

    def outer_piece(k, to, cc):
        return remote(
            volume.at[to - 1 + 2 * cc], planes.at[2 * cc, me], osend.at[k], orecv.at[me],
            {"gx": to},
        )

    def chunk(slot, zz, yy):
        return planes.at[slot, pl.ds(zz * 4 + yy * 2, 2)]

    def to_partner(zz, yy):
        return remote(
            chunk(1, zz, yy), chunk(2 * core, zz, yy), psend.at[zz, yy], precv.at[zz, yy],
            {"gx": partner},
        )

    def to_outer(zz):
        return remote(
            chunk(1, zz, row), chunk(2 - 2 * core, zz, row), hsend.at[zz], hrecv.at[zz],
            {"gx": outer},
        )

    order = [d for pair in zip(range(1, count // 2), range(count - 1, count // 2, -1)) for d in pair]
    order = [count // 2] + order[::-1]

    for g in range(2):
        @pl.when(group == g)
        def _(g=g):
            for j in range(half):
                direct(g, j).start()

    for d in order:
        piece(d).start()
    own_volume.start()
    for k, to, cc in mates():
        @pl.when((to > 0) & (to < count - 1))
        def _(k=k, to=to, cc=cc):
            outer_piece(k, to, cc).start()

    @pl.when(inner)
    def _():
        own_outer().start()

    for q in range(2):
        beside(q, chip, True).start()
    own_weight.start()
    own_bias.start()

    @pl.when(me == 0)
    def _():
        planes[0] = jnp.zeros(planes.shape[1:], planes.dtype)

    @pl.when(me == count - 1)
    def _():
        planes[2] = jnp.zeros(planes.shape[1:], planes.dtype)
        hidden[1] = jnp.zeros(hidden.shape[1:], hidden.dtype)

    for g in range(2):
        @pl.when(group == g)
        def _(g=g):
            for i, c in enumerate(others):
                arrived(shard(c * 2 + core, g), wrecv.at[g, c])
                if i == 0:
                    for j in range(1, half):
                        relay(g, j).start()
                across(g, c).start()
                beside(g, c).start()

    own_volume.wait()
    chunks = [((bed + db) % beds, yy) for yy in (row, 1 - row) for db in range(beds)]
    for i, (zz, yy) in enumerate(chunks):
        for cc in range(2):
            src = zz * 4 + yy * 2 + cc

            @pl.when(src != me)
            def _(src=src):
                arrived(planes.at[1, src], vrecv.at[src])

        to_partner(zz, yy).start()
        if i < beds:
            @pl.when(inner)
            def _(zz=zz):
                to_outer(zz).start()

    for g in range(2):
        @pl.when(group == g)
        def _(g=g):
            for c in others:
                arrived(shard(c * 2 + core, 1 - g), wrecv.at[1 - g, c])
                beside(1 - g, c).start()

    own_weight.wait()
    own_bias.wait()

    @pl.when(inner)
    def _():
        own_outer().wait()
        for k, src, cc in mates():
            arrived(planes.at[2 * core, src], orecv.at[src])
        for zz in range(beds):
            arrived(chunk(2 * core, zz, 1 - row), hrecv.at[zz])

    for zz, yy in chunks:
        arrived(chunk(2 - 2 * core, zz, yy), precv.at[zz, yy])
    for c in [chip] + others:
        for q in range(2):
            arrived(shard(c * 2 + 1 - core, q), crecv.at[q, c])

    cin = count * volume.shape[2]
    cells = [lambda y, kx=kx: planes[kx, :, y].reshape(cin, wide_z) for kx in range(3)]
    hidden[0] = conv_hidden(
        cells, wide_y, wide_z, lambda t: weights[:, t].reshape(cin, weights.shape[3]),
        jnp.transpose(jnp.broadcast_to(bias_row[...], (wide_z, bias_row.shape[1]))),
    )

    def edge():
        return remote(hidden.at[0], hidden.at[1], esend, erecv, {"gx": me - 1})

    @pl.when(me > 0)
    def _():
        edge().start()

    for d in order:
        piece(d).wait_send()
    for k, to, cc in mates():
        @pl.when((to > 0) & (to < count - 1))
        def _(k=k, to=to, cc=cc):
            outer_piece(k, to, cc).wait_send()

    for zz, yy in chunks:
        to_partner(zz, yy).wait_send()

    @pl.when(inner)
    def _():
        for zz in range(beds):
            to_outer(zz).wait_send()

    for g in range(2):
        @pl.when(group == g)
        def _(g=g):
            for j in range(half):
                direct(g, j).wait_send()
            for j in range(1, half):
                relay(g, j).wait_send()
            for c in others:
                across(g, c).wait_send()

    for q in range(2):
        beside(q, chip, True).wait_send()
        for c in others:
            beside(q, c).wait_send()

    @pl.when(me < count - 1)
    def _():
        arrived(hidden.at[1], erecv)

    @pl.when(me > 0)
    def _():
        edge().wait_send()

    hidden_out[...] = hidden[...]


def local_conv(planes, weight, bias, hidden_out):
    wide_y, wide_z = planes.shape[1], planes.shape[3]
    cells = [lambda y, kx=kx: planes[kx, y] for kx in range(3)]
    hidden_out[...] = conv_hidden(cells, wide_y, wide_z, lambda t: weight[t], bias[...])


def transposed(hidden, tconv, out):
    wide_z = out.shape[3] // 2
    wide_y = out.shape[1] // 2
    cup = tconv.shape[1]
    cout = tconv.shape[2]
    here, after = hidden[0], hidden[1]

    def down(x):
        return jnp.concatenate([x[:, wide_z:], jnp.zeros_like(x[:, :wide_z])], axis=1)

    def taps(kx, ky):
        t = kx * 9 + ky * 3
        return tconv[t : t + 3].reshape(3 * cup, cout)

    row = lax.broadcasted_iota(jnp.int32, (2 * wide_z, 2 * wide_z), 0)
    col = lax.broadcasted_iota(jnp.int32, (2 * wide_z, 2 * wide_z), 1)
    spread = jnp.where(
        col == jnp.where(row < wide_z, 2 * row, 2 * (row - wide_z) + 1), 1.0, 0.0
    ).astype(jnp.bfloat16)
    x_options = (((1, here),), ((2, here), (0, after)))
    for pu in range(2):
        for pv in range(2):
            left, right = [], []
            for kx, field in x_options[pu]:
                for ky, shifted in (((1, False),), ((2, False), (0, True)))[pv]:
                    left.append(taps(kx, ky))
                    right.append(down(field) if shifted else field)
            product = jnp.dot(
                jnp.concatenate(left, axis=1), jnp.concatenate(right, axis=0),
                preferred_element_type=jnp.float32,
            )
            pairs = []
            for y in range(wide_y):
                part = product[:, y * wide_z : (y + 1) * wide_z]
                even = part[cup : 2 * cup]
                odd = part[2 * cup :] + shift_down(part[:cup])
                pairs.append(jnp.concatenate([even, odd], axis=1).astype(jnp.bfloat16))
            mixed = jnp.dot(
                jnp.concatenate(pairs, axis=0), spread, preferred_element_type=jnp.float32
            ).astype(jnp.bfloat16)
            for y in range(wide_y):
                out[pu, 2 * y + pv] = mixed[y * cup : (y + 1) * cup]


def native_hidden(volume, conv_weight, bias):
    count = lax.axis_size("gx")
    forward = [(i, i + 1) for i in range(count - 1)]
    backward = [(i + 1, i) for i in range(count - 1)]
    local = lax.all_to_all(volume, "gx", split_axis=0, concat_axis=1, tiled=True)
    weight = lax.all_gather(conv_weight, "gx", axis=0, tiled=True)
    rows = local.shape[0]
    low = lax.ppermute(local[rows - 1 :], "gx", forward)
    high = lax.ppermute(local[:1], "gx", backward)
    planes = jnp.transpose(jnp.concatenate([low, local, high], axis=0), (0, 2, 1, 3))
    weight = jnp.transpose(weight, (1, 0, 2))
    cout = weight.shape[2]
    shape = jax.ShapeDtypeStruct((cout, planes.shape[1] * planes.shape[3]), jnp.bfloat16)
    conv = pl.pallas_call(
        local_conv, out_shape=shape, in_specs=[VMEM] * 3, out_specs=VMEM,
        compiler_params=pltpu.CompilerParams(vmem_limit_bytes=40 << 20),
    )
    hidden = [conv(planes[r : r + 3], weight, bias) for r in range(rows)]
    hidden.append(lax.ppermute(hidden[0], "gx", backward))
    return [jnp.stack(hidden[r : r + 2]) for r in range(rows)]


def remote_hidden(volume, conv_weight, bias):
    count = lax.axis_size("gx")
    chips = count // 2
    cells = jnp.transpose(volume, (0, 2, 1, 3))
    weight = jnp.transpose(conv_weight, (1, 0, 2))
    cout = weight.shape[2]
    lanes = cells.shape[1] * cells.shape[3]
    dma = pltpu.SemaphoreType.DMA
    hidden = pl.pallas_call(
        exchange_conv,
        out_shape=jax.ShapeDtypeStruct((2, cout, lanes), jnp.bfloat16),
        in_specs=[HBM, HBM, HBM],
        out_specs=VMEM,
        scratch_shapes=[
            pltpu.VMEM((3, count) + cells.shape[1:], jnp.bfloat16),
            pltpu.VMEM((count,) + weight.shape, jnp.bfloat16),
            pltpu.VMEM((2, cout, lanes), jnp.bfloat16),
            pltpu.VMEM((1, cout), jnp.float32),
            dma((4,)),
            dma((count,)), dma((count,)), dma((chips,)), dma((count,)),
            dma((count // 4,)), dma((count // 4,)), dma((count // 4, 2)), dma((count // 4, 2)),
            dma((chips,)), dma((chips,)), dma((2, chips)), dma((chips,)),
            dma((2, chips)), dma((2, chips)),
            dma(()), dma(()),
        ],
        compiler_params=pltpu.CompilerParams(
            collective_id=0, has_side_effects=True, vmem_limit_bytes=40 << 20
        ),
    )(cells, weight, bias.reshape(1, cout))
    return [hidden]


def per_device(volume, conv_weight, conv_bias, tconv_weight):
    count = lax.axis_size("gx")
    rows = volume.shape[0] // count
    bias = conv_bias[:, None]
    suited = (
        rows == 1 and count == 16 and lax.axis_size("groups") == 2
        and volume.shape[1] % 16 == 0
    )
    hidden = (remote_hidden if suited else native_hidden)(volume, conv_weight, bias)
    cup = tconv_weight.shape[1]
    shape = jax.ShapeDtypeStruct(
        (2, 2 * volume.shape[2], cup, 2 * volume.shape[3]), jnp.bfloat16
    )
    tconv = pl.pallas_call(
        transposed, out_shape=shape, in_specs=[VMEM] * 2, out_specs=VMEM,
        compiler_params=pltpu.CompilerParams(vmem_limit_bytes=40 << 20),
    )
    outs = [tconv(planes, tconv_weight) for planes in hidden]
    out = outs[0] if len(outs) == 1 else jnp.concatenate(outs, axis=0)
    return jnp.transpose(out, (0, 2, 1, 3))


def solution(mesh):
    return jax.shard_map(
        per_device,
        mesh=mesh,
        in_specs=(P("groups", "gx", None, None), P("gx", None, None), P(), P()),
        out_specs=P(("groups", "gx"), None, None, None),
        check_vma=False,
    )
```

```python
import jax
import jax.numpy as jnp
from jax import lax
from jax.experimental import pallas as pl
from jax.experimental.pallas import tpu as pltpu
from jax.sharding import PartitionSpec as P

MESH = pl.DeviceIdType.MESH
VMEM = pl.BlockSpec(memory_space=pltpu.VMEM)
HBM = pl.BlockSpec(memory_space=pltpu.HBM)


def shift_up(block):
    lane = lax.broadcasted_iota(jnp.int32, block.shape, 1)
    return jnp.where(lane == 0, 0.0, pltpu.roll(block, 1, axis=1))


def shift_down(block):
    size = block.shape[1]
    lane = lax.broadcasted_iota(jnp.int32, block.shape, 1)
    return jnp.where(lane == size - 1, 0.0, pltpu.roll(block, size - 1, axis=1))


def conv_hidden(planes, wide_y, wide_z, tap, bias):
    zero = jnp.zeros_like(planes[0](0))
    total = None
    for kx in range(3):
        padded = jnp.concatenate(
            [zero] + [planes[kx](y) for y in range(wide_y)] + [zero], axis=1
        )
        for ky in range(3):
            weight = jnp.concatenate([tap(kx * 9 + ky * 3 + kz) for kz in range(3)], axis=1)
            cells = padded[:, ky * wide_z : (ky + wide_y) * wide_z]
            term = lax.dot_general(
                weight, cells, (((0,), (0,)), ((), ())), preferred_element_type=jnp.float32
            )
            total = term if total is None else total + term
    cout = total.shape[0] // 3
    rows = []
    for y in range(wide_y):
        part = total[:, y * wide_z : (y + 1) * wide_z]
        rows.append(
            part[cout : 2 * cout]
            + shift_up(part[:cout])
            + shift_down(part[2 * cout :])
            + bias
        )
    return jnp.maximum(jnp.concatenate(rows, axis=1), 0.0).astype(jnp.bfloat16)


def exchange_conv(volume, weight, bias, tconv, out, planes, weights, hidden, bias_row, tconv_rows, entry_sem,
                  vsend, vrecv, osend, orecv, hsend, hrecv, psend, precv,
                  wsend, rsend, wrecv, xsend, csend, crecv, esend, erecv):
    me = lax.axis_index("gx")
    count = lax.axis_size("gx")
    group = lax.axis_index("groups")
    chips = count // 2
    chip, core = me // 2, me % 2
    beds = count // 4
    bed, row = me // 4, chip % 2
    partner = me + 1 - 2 * core
    wide_y, wide_z = volume.shape[1], volume.shape[3]
    taps = weight.shape[0]
    cuts = ((0, (taps + 1) // 2), ((taps + 1) // 2, taps // 2))

    barrier = pltpu.get_barrier_semaphore()
    for d in range(1, count):
        pl.semaphore_signal(
            barrier, inc=1, device_id={"gx": (me + d) % count}, device_id_type=MESH
        )
    pl.semaphore_signal(barrier, inc=1, device_id={"groups": 1 - group}, device_id_type=MESH)
    pl.semaphore_wait(barrier, count)

    def remote(src, dst, send, recv, target):
        return pltpu.make_async_remote_copy(
            src_ref=src, dst_ref=dst, send_sem=send, recv_sem=recv,
            device_id=target, device_id_type=MESH,
        )

    def arrived(at, sem):
        pltpu.make_async_copy(at, at, sem).wait()

    inner = (me > 0) & (me < count - 1)
    outer = me - 1 + 2 * core
    own_volume = pltpu.make_async_copy(volume.at[me], planes.at[1, me], entry_sem.at[0])
    own_weight = pltpu.make_async_copy(weight, weights.at[me], entry_sem.at[1])
    own_bias = pltpu.make_async_copy(bias, bias_row, entry_sem.at[2])

    own_tconv = pltpu.make_async_copy(tconv, tconv_rows, entry_sem.at[4])

    def own_outer():
        return pltpu.make_async_copy(
            volume.at[outer], planes.at[2 * core, me], entry_sem.at[3]
        )

    half = chips // 2
    place = chip % half
    base = chip - place
    mirror = (chip + half) % chips

    def near(j):
        return base + (place + j) % half

    def far(j):
        return (half - base) + (place + j) % half

    others = [mirror] + [near(j) for j in range(1, half)] + [far(j) for j in range(1, half)]

    def shard(slot, q):
        return weights.at[slot, pl.ds(*cuts[q])]

    def direct(q, j):
        to = mirror if j == 0 else near(j)
        return remote(
            weight.at[pl.ds(*cuts[q])], shard(me, q), wsend.at[j], wrecv.at[q, chip],
            {"gx": to * 2 + core},
        )

    def relay(q, j):
        at = shard(mirror * 2 + core, q)
        return remote(at, at, rsend.at[j], wrecv.at[q, mirror], {"gx": near(j) * 2 + core})

    def across(q, c):
        at = shard(c * 2 + core, q)
        return remote(at, at, xsend.at[c], wrecv.at[q, c], {"groups": 1 - group})

    def beside(q, c, own=False):
        at = shard(c * 2 + core, q)
        src = weight.at[pl.ds(*cuts[q])] if own else at
        return remote(src, at, csend.at[q, c], crecv.at[q, c], {"gx": partner})

    def piece(d):
        to = (me + d) % count
        return remote(volume.at[to], planes.at[1, me], vsend.at[d], vrecv.at[me], {"gx": to})

    def mates():
        found = [(0, partner, 1 - core)]
        for db in range(1, beds):
            for cc in range(2):
                found.append((2 * db + cc, ((bed + db) % beds) * 4 + row * 2 + cc, cc))
        return found

    def outer_piece(k, to, cc):
        return remote(
            volume.at[to - 1 + 2 * cc], planes.at[2 * cc, me], osend.at[k], orecv.at[me],
            {"gx": to},
        )

    def chunk(slot, zz, yy):
        return planes.at[slot, pl.ds(zz * 4 + yy * 2, 2)]

    def to_partner(zz, yy):
        return remote(
            chunk(1, zz, yy), chunk(2 * core, zz, yy), psend.at[zz, yy], precv.at[zz, yy],
            {"gx": partner},
        )

    def to_outer(zz):
        return remote(
            chunk(1, zz, row), chunk(2 - 2 * core, zz, row), hsend.at[zz], hrecv.at[zz],
            {"gx": outer},
        )

    order = [d for pair in zip(range(1, count // 2), range(count - 1, count // 2, -1)) for d in pair]
    order = [count // 2] + order[::-1]

    for g in range(2):
        @pl.when(group == g)
        def _(g=g):
            for j in range(half):
                direct(g, j).start()

    for d in order:
        piece(d).start()
    own_volume.start()
    for k, to, cc in mates():
        @pl.when((to > 0) & (to < count - 1))
        def _(k=k, to=to, cc=cc):
            outer_piece(k, to, cc).start()

    @pl.when(inner)
    def _():
        own_outer().start()

    for q in range(2):
        beside(q, chip, True).start()
    own_weight.start()
    own_bias.start()
    own_tconv.start()

    @pl.when(me == 0)
    def _():
        planes[0] = jnp.zeros(planes.shape[1:], planes.dtype)

    @pl.when(me == count - 1)
    def _():
        planes[2] = jnp.zeros(planes.shape[1:], planes.dtype)
        hidden[1] = jnp.zeros(hidden.shape[1:], hidden.dtype)

    for g in range(2):
        @pl.when(group == g)
        def _(g=g):
            for i, c in enumerate(others):
                arrived(shard(c * 2 + core, g), wrecv.at[g, c])
                if i == 0:
                    for j in range(1, half):
                        relay(g, j).start()
                across(g, c).start()
                beside(g, c).start()

    own_volume.wait()
    chunks = [((bed + db) % beds, yy) for yy in (row, 1 - row) for db in range(beds)]
    for i, (zz, yy) in enumerate(chunks):
        for cc in range(2):
            src = zz * 4 + yy * 2 + cc

            @pl.when(src != me)
            def _(src=src):
                arrived(planes.at[1, src], vrecv.at[src])

        to_partner(zz, yy).start()
        if i < beds:
            @pl.when(inner)
            def _(zz=zz):
                to_outer(zz).start()

    for g in range(2):
        @pl.when(group == g)
        def _(g=g):
            for c in others:
                arrived(shard(c * 2 + core, 1 - g), wrecv.at[1 - g, c])
                beside(1 - g, c).start()

    own_weight.wait()
    own_bias.wait()

    @pl.when(inner)
    def _():
        own_outer().wait()
        for k, src, cc in mates():
            arrived(planes.at[2 * core, src], orecv.at[src])
        for zz in range(beds):
            arrived(chunk(2 * core, zz, 1 - row), hrecv.at[zz])

    for zz, yy in chunks:
        arrived(chunk(2 - 2 * core, zz, yy), precv.at[zz, yy])
    for c in [chip] + others:
        for q in range(2):
            arrived(shard(c * 2 + 1 - core, q), crecv.at[q, c])

    cin = count * volume.shape[2]
    cells = [lambda y, kx=kx: planes[kx, :, y].reshape(cin, wide_z) for kx in range(3)]
    hidden[0] = conv_hidden(
        cells, wide_y, wide_z, lambda t: weights[:, t].reshape(cin, weights.shape[3]),
        jnp.transpose(jnp.broadcast_to(bias_row[...], (wide_z, bias_row.shape[1]))),
    )

    def edge():
        return remote(hidden.at[0], hidden.at[1], esend, erecv, {"gx": me - 1})

    @pl.when(me > 0)
    def _():
        edge().start()

    own_tconv.wait()
    decode(hidden, tconv_rows, out, 0)

    for d in order:
        piece(d).wait_send()
    for k, to, cc in mates():
        @pl.when((to > 0) & (to < count - 1))
        def _(k=k, to=to, cc=cc):
            outer_piece(k, to, cc).wait_send()

    for zz, yy in chunks:
        to_partner(zz, yy).wait_send()

    @pl.when(inner)
    def _():
        for zz in range(beds):
            to_outer(zz).wait_send()

    for g in range(2):
        @pl.when(group == g)
        def _(g=g):
            for j in range(half):
                direct(g, j).wait_send()
            for j in range(1, half):
                relay(g, j).wait_send()
            for c in others:
                across(g, c).wait_send()

    for q in range(2):
        beside(q, chip, True).wait_send()
        for c in others:
            beside(q, c).wait_send()

    @pl.when(me < count - 1)
    def _():
        arrived(hidden.at[1], erecv)

    @pl.when(me > 0)
    def _():
        edge().wait_send()

    decode(hidden, tconv_rows, out, 1)


def local_conv(planes, weight, bias, hidden_out):
    wide_y, wide_z = planes.shape[1], planes.shape[3]
    cells = [lambda y, kx=kx: planes[kx, y] for kx in range(3)]
    hidden_out[...] = conv_hidden(cells, wide_y, wide_z, lambda t: weight[t], bias[...])


def transposed(hidden, tconv, out):
    decode(hidden, tconv, out, 0)
    decode(hidden, tconv, out, 1)


def decode(hidden, tconv, out, pu):
    wide_z = out.shape[3] // 2
    wide_y = out.shape[1] // 2
    cup = tconv.shape[1]
    cout = tconv.shape[2]

    def down(x):
        return jnp.concatenate([x[:, wide_z:], jnp.zeros_like(x[:, :wide_z])], axis=1)

    def taps(kx, ky):
        t = kx * 9 + ky * 3
        return tconv[t : t + 3].reshape(3 * cup, cout)

    row = lax.broadcasted_iota(jnp.int32, (2 * wide_z, 2 * wide_z), 0)
    col = lax.broadcasted_iota(jnp.int32, (2 * wide_z, 2 * wide_z), 1)
    spread = jnp.where(
        col == jnp.where(row < wide_z, 2 * row, 2 * (row - wide_z) + 1), 1.0, 0.0
    ).astype(jnp.bfloat16)
    x_options = ((1, 0),) if pu == 0 else ((2, 0), (0, 1))
    for pv in range(2):
        left, right = [], []
        for kx, at in x_options:
            field = hidden[at]
            for ky, shifted in (((1, False),), ((2, False), (0, True)))[pv]:
                left.append(taps(kx, ky))
                right.append(down(field) if shifted else field)
        product = jnp.dot(
            jnp.concatenate(left, axis=1), jnp.concatenate(right, axis=0),
            preferred_element_type=jnp.float32,
        )
        pairs = []
        for y in range(wide_y):
            part = product[:, y * wide_z : (y + 1) * wide_z]
            even = part[cup : 2 * cup]
            odd = part[2 * cup :] + shift_down(part[:cup])
            pairs.append(jnp.concatenate([even, odd], axis=1).astype(jnp.bfloat16))
        mixed = jnp.dot(
            jnp.concatenate(pairs, axis=0), spread, preferred_element_type=jnp.float32
        ).astype(jnp.bfloat16)
        for y in range(wide_y):
            out[pu, 2 * y + pv] = mixed[y * cup : (y + 1) * cup]


def native_hidden(volume, conv_weight, bias):
    count = lax.axis_size("gx")
    forward = [(i, i + 1) for i in range(count - 1)]
    backward = [(i + 1, i) for i in range(count - 1)]
    local = lax.all_to_all(volume, "gx", split_axis=0, concat_axis=1, tiled=True)
    weight = lax.all_gather(conv_weight, "gx", axis=0, tiled=True)
    rows = local.shape[0]
    low = lax.ppermute(local[rows - 1 :], "gx", forward)
    high = lax.ppermute(local[:1], "gx", backward)
    planes = jnp.transpose(jnp.concatenate([low, local, high], axis=0), (0, 2, 1, 3))
    weight = jnp.transpose(weight, (1, 0, 2))
    cout = weight.shape[2]
    shape = jax.ShapeDtypeStruct((cout, planes.shape[1] * planes.shape[3]), jnp.bfloat16)
    conv = pl.pallas_call(
        local_conv, out_shape=shape, in_specs=[VMEM] * 3, out_specs=VMEM,
        compiler_params=pltpu.CompilerParams(vmem_limit_bytes=40 << 20),
    )
    hidden = [conv(planes[r : r + 3], weight, bias) for r in range(rows)]
    hidden.append(lax.ppermute(hidden[0], "gx", backward))
    return [jnp.stack(hidden[r : r + 2]) for r in range(rows)]


def remote_decoded(volume, conv_weight, bias, tconv_weight, shape):
    count = lax.axis_size("gx")
    chips = count // 2
    cells = jnp.transpose(volume, (0, 2, 1, 3))
    weight = jnp.transpose(conv_weight, (1, 0, 2))
    cout = weight.shape[2]
    lanes = cells.shape[1] * cells.shape[3]
    dma = pltpu.SemaphoreType.DMA
    return pl.pallas_call(
        exchange_conv,
        out_shape=shape,
        in_specs=[HBM] * 4,
        out_specs=VMEM,
        scratch_shapes=[
            pltpu.VMEM((3, count) + cells.shape[1:], jnp.bfloat16),
            pltpu.VMEM((count,) + weight.shape, jnp.bfloat16),
            pltpu.VMEM((2, cout, lanes), jnp.bfloat16),
            pltpu.VMEM((1, cout), jnp.float32),
            pltpu.VMEM(tconv_weight.shape, jnp.bfloat16),
            dma((5,)),
            dma((count,)), dma((count,)), dma((chips,)), dma((count,)),
            dma((count // 4,)), dma((count // 4,)), dma((count // 4, 2)), dma((count // 4, 2)),
            dma((chips,)), dma((chips,)), dma((2, chips)), dma((chips,)),
            dma((2, chips)), dma((2, chips)),
            dma(()), dma(()),
        ],
        compiler_params=pltpu.CompilerParams(
            collective_id=0, has_side_effects=True, vmem_limit_bytes=60 << 20
        ),
    )(cells, weight, bias.reshape(1, cout), tconv_weight)


def per_device(volume, conv_weight, conv_bias, tconv_weight):
    count = lax.axis_size("gx")
    rows = volume.shape[0] // count
    bias = conv_bias[:, None]
    suited = (
        rows == 1 and count == 16 and lax.axis_size("groups") == 2
        and volume.shape[1] % 16 == 0
    )
    cup = tconv_weight.shape[1]
    shape = jax.ShapeDtypeStruct(
        (2, 2 * volume.shape[2], cup, 2 * volume.shape[3]), jnp.bfloat16
    )
    if suited:
        out = remote_decoded(volume, conv_weight, bias, tconv_weight, shape)
    else:
        tconv = pl.pallas_call(
            transposed, out_shape=shape, in_specs=[VMEM] * 2, out_specs=VMEM,
            compiler_params=pltpu.CompilerParams(vmem_limit_bytes=40 << 20),
        )
        hidden = native_hidden(volume, conv_weight, bias)
        outs = [tconv(planes, tconv_weight) for planes in hidden]
        out = outs[0] if len(outs) == 1 else jnp.concatenate(outs, axis=0)
    return jnp.transpose(out, (0, 2, 1, 3))


def solution(mesh):
    return jax.shard_map(
        per_device,
        mesh=mesh,
        in_specs=(P("groups", "gx", None, None), P("gx", None, None), P(), P()),
        out_specs=P(("groups", "gx"), None, None, None),
        check_vma=False,
    )
```

```python
import jax
import jax.numpy as jnp
from jax import lax
from jax.experimental import pallas as pl
from jax.experimental.pallas import tpu as pltpu
from jax.sharding import PartitionSpec as P

MESH = pl.DeviceIdType.MESH
VMEM = pl.BlockSpec(memory_space=pltpu.VMEM)
HBM = pl.BlockSpec(memory_space=pltpu.HBM)


def shift_up(block):
    lane = lax.broadcasted_iota(jnp.int32, block.shape, 1)
    return jnp.where(lane == 0, 0.0, pltpu.roll(block, 1, axis=1))


def shift_down(block):
    size = block.shape[1]
    lane = lax.broadcasted_iota(jnp.int32, block.shape, 1)
    return jnp.where(lane == size - 1, 0.0, pltpu.roll(block, size - 1, axis=1))


def conv_hidden(planes, wide_y, wide_z, tap, bias):
    zero = jnp.zeros_like(planes[0](0))
    total = None
    for kx in range(3):
        padded = jnp.concatenate(
            [zero] + [planes[kx](y) for y in range(wide_y)] + [zero], axis=1
        )
        for ky in range(3):
            weight = jnp.concatenate([tap(kx * 9 + ky * 3 + kz) for kz in range(3)], axis=1)
            cells = padded[:, ky * wide_z : (ky + wide_y) * wide_z]
            term = lax.dot_general(
                weight, cells, (((0,), (0,)), ((), ())), preferred_element_type=jnp.float32
            )
            total = term if total is None else total + term
    cout = total.shape[0] // 3
    rows = []
    for y in range(wide_y):
        part = total[:, y * wide_z : (y + 1) * wide_z]
        rows.append(
            part[cout : 2 * cout]
            + shift_up(part[:cout])
            + shift_down(part[2 * cout :])
            + bias
        )
    return jnp.maximum(jnp.concatenate(rows, axis=1), 0.0).astype(jnp.bfloat16)


def exchange_conv(volume, weight, bias, hidden_out, planes, weights, hidden, bias_row, entry_sem,
                  vsend, vrecv, osend, orecv, hsend, hrecv, psend, precv,
                  wsend, rsend, wrecv, xsend, csend, crecv, esend, erecv):
    me = lax.axis_index("gx")
    count = lax.axis_size("gx")
    group = lax.axis_index("groups")
    chips = count // 2
    chip, core = me // 2, me % 2
    beds = count // 4
    bed, row = me // 4, chip % 2
    partner = me + 1 - 2 * core
    wide_y, wide_z = volume.shape[1], volume.shape[3]
    taps = weight.shape[0]
    cuts = ((0, (taps + 1) // 2), ((taps + 1) // 2, taps // 2))

    barrier = pltpu.get_barrier_semaphore()
    for d in range(1, count):
        pl.semaphore_signal(
            barrier, inc=1, device_id={"gx": (me + d) % count}, device_id_type=MESH
        )
    pl.semaphore_signal(barrier, inc=1, device_id={"groups": 1 - group}, device_id_type=MESH)
    pl.semaphore_wait(barrier, count)

    def remote(src, dst, send, recv, target):
        return pltpu.make_async_remote_copy(
            src_ref=src, dst_ref=dst, send_sem=send, recv_sem=recv,
            device_id=target, device_id_type=MESH,
        )

    def arrived(at, sem):
        pltpu.make_async_copy(at, at, sem).wait()

    inner = (me > 0) & (me < count - 1)
    outer = me - 1 + 2 * core
    own_volume = pltpu.make_async_copy(volume.at[me], planes.at[1, me], entry_sem.at[0])
    own_weight = pltpu.make_async_copy(weight, weights.at[me], entry_sem.at[1])
    own_bias = pltpu.make_async_copy(bias, bias_row, entry_sem.at[2])

    def own_outer():
        return pltpu.make_async_copy(
            volume.at[outer], planes.at[2 * core, me], entry_sem.at[3]
        )

    half = chips // 2
    place = chip % half
    base = chip - place
    mirror = (chip + half) % chips

    def near(j):
        return base + (place + j) % half

    def far(j):
        return (half - base) + (place + j) % half

    others = [mirror] + [near(j) for j in range(1, half)] + [far(j) for j in range(1, half)]

    def shard(slot, q):
        return weights.at[slot, pl.ds(*cuts[q])]

    def direct(q, j):
        to = mirror if j == 0 else near(j)
        return remote(
            weight.at[pl.ds(*cuts[q])], shard(me, q), wsend.at[j], wrecv.at[q, chip],
            {"gx": to * 2 + core},
        )

    def relay(q, j):
        at = shard(mirror * 2 + core, q)
        return remote(at, at, rsend.at[j], wrecv.at[q, mirror], {"gx": near(j) * 2 + core})

    def across(q, c):
        at = shard(c * 2 + core, q)
        return remote(at, at, xsend.at[c], wrecv.at[q, c], {"groups": 1 - group})

    def beside(q, c, own=False):
        at = shard(c * 2 + core, q)
        src = weight.at[pl.ds(*cuts[q])] if own else at
        return remote(src, at, csend.at[q, c], crecv.at[q, c], {"gx": partner})

    def piece(d):
        to = (me + d) % count
        return remote(volume.at[to], planes.at[1, me], vsend.at[d], vrecv.at[me], {"gx": to})

    def mates():
        found = [(0, partner, 1 - core)]
        for db in range(1, beds):
            for cc in range(2):
                found.append((2 * db + cc, ((bed + db) % beds) * 4 + row * 2 + cc, cc))
        return found

    def outer_piece(k, to, cc):
        return remote(
            volume.at[to - 1 + 2 * cc], planes.at[2 * cc, me], osend.at[k], orecv.at[me],
            {"gx": to},
        )

    def chunk(slot, zz, yy):
        return planes.at[slot, pl.ds(zz * 4 + yy * 2, 2)]

    def to_partner(zz, yy):
        return remote(
            chunk(1, zz, yy), chunk(2 * core, zz, yy), psend.at[zz, yy], precv.at[zz, yy],
            {"gx": partner},
        )

    def to_outer(zz):
        return remote(
            chunk(1, zz, row), chunk(2 - 2 * core, zz, row), hsend.at[zz], hrecv.at[zz],
            {"gx": outer},
        )

    order = [d for pair in zip(range(1, count // 2), range(count - 1, count // 2, -1)) for d in pair]
    order = [count // 2] + order[::-1]

    for g in range(2):
        @pl.when(group == g)
        def _(g=g):
            for j in range(half):
                direct(g, j).start()

    own_volume.start()
    @pl.when(inner)
    def _():
        own_outer().start()

    for q in range(2):
        beside(q, chip, True).start()
    own_weight.start()
    own_bias.start()

    @pl.when(me == 0)
    def _():
        planes[0] = jnp.zeros(planes.shape[1:], planes.dtype)

    @pl.when(me == count - 1)
    def _():
        planes[2] = jnp.zeros(planes.shape[1:], planes.dtype)
        hidden[1] = jnp.zeros(hidden.shape[1:], hidden.dtype)

    for g in range(2):
        @pl.when(group == g)
        def _(g=g):
            for i, c in enumerate(others):
                arrived(shard(c * 2 + core, g), wrecv.at[g, c])
                if i == 0:
                    for j in range(1, half):
                        relay(g, j).start()
                    for d in order:
                        piece(d).start()
                across(g, c).start()
                beside(g, c).start()

    for k, to, cc in mates():
        @pl.when((to > 0) & (to < count - 1))
        def _(k=k, to=to, cc=cc):
            outer_piece(k, to, cc).start()

    own_volume.wait()
    chunks = [((bed + db) % beds, yy) for yy in (row, 1 - row) for db in range(beds)]
    for i, (zz, yy) in enumerate(chunks):
        for cc in range(2):
            src = zz * 4 + yy * 2 + cc

            @pl.when(src != me)
            def _(src=src):
                arrived(planes.at[1, src], vrecv.at[src])

        to_partner(zz, yy).start()
        if i < beds:
            @pl.when(inner)
            def _(zz=zz):
                to_outer(zz).start()

    for g in range(2):
        @pl.when(group == g)
        def _(g=g):
            for c in others:
                arrived(shard(c * 2 + core, 1 - g), wrecv.at[1 - g, c])
                beside(1 - g, c).start()

    own_weight.wait()
    own_bias.wait()

    @pl.when(inner)
    def _():
        own_outer().wait()
        for k, src, cc in mates():
            arrived(planes.at[2 * core, src], orecv.at[src])
        for zz in range(beds):
            arrived(chunk(2 * core, zz, 1 - row), hrecv.at[zz])

    for zz, yy in chunks:
        arrived(chunk(2 - 2 * core, zz, yy), precv.at[zz, yy])
    for c in [chip] + others:
        for q in range(2):
            arrived(shard(c * 2 + 1 - core, q), crecv.at[q, c])

    cin = count * volume.shape[2]
    cells = [lambda y, kx=kx: planes[kx, :, y].reshape(cin, wide_z) for kx in range(3)]
    hidden[0] = conv_hidden(
        cells, wide_y, wide_z, lambda t: weights[:, t].reshape(cin, weights.shape[3]),
        jnp.transpose(jnp.broadcast_to(bias_row[...], (wide_z, bias_row.shape[1]))),
    )

    def edge():
        return remote(hidden.at[0], hidden.at[1], esend, erecv, {"gx": me - 1})

    @pl.when(me > 0)
    def _():
        edge().start()

    for d in order:
        piece(d).wait_send()
    for k, to, cc in mates():
        @pl.when((to > 0) & (to < count - 1))
        def _(k=k, to=to, cc=cc):
            outer_piece(k, to, cc).wait_send()

    for zz, yy in chunks:
        to_partner(zz, yy).wait_send()

    @pl.when(inner)
    def _():
        for zz in range(beds):
            to_outer(zz).wait_send()

    for g in range(2):
        @pl.when(group == g)
        def _(g=g):
            for j in range(half):
                direct(g, j).wait_send()
            for j in range(1, half):
                relay(g, j).wait_send()
            for c in others:
                across(g, c).wait_send()

    for q in range(2):
        beside(q, chip, True).wait_send()
        for c in others:
            beside(q, c).wait_send()

    @pl.when(me < count - 1)
    def _():
        arrived(hidden.at[1], erecv)

    @pl.when(me > 0)
    def _():
        edge().wait_send()

    hidden_out[...] = hidden[...]


def local_conv(planes, weight, bias, hidden_out):
    wide_y, wide_z = planes.shape[1], planes.shape[3]
    cells = [lambda y, kx=kx: planes[kx, y] for kx in range(3)]
    hidden_out[...] = conv_hidden(cells, wide_y, wide_z, lambda t: weight[t], bias[...])


def transposed(hidden, tconv, out):
    wide_z = out.shape[3] // 2
    wide_y = out.shape[1] // 2
    cup = tconv.shape[1]
    cout = tconv.shape[2]
    here, after = hidden[0], hidden[1]

    def down(x):
        return jnp.concatenate([x[:, wide_z:], jnp.zeros_like(x[:, :wide_z])], axis=1)

    def taps(kx, ky):
        t = kx * 9 + ky * 3
        return tconv[t : t + 3].reshape(3 * cup, cout)

    row = lax.broadcasted_iota(jnp.int32, (2 * wide_z, 2 * wide_z), 0)
    col = lax.broadcasted_iota(jnp.int32, (2 * wide_z, 2 * wide_z), 1)
    spread = jnp.where(
        col == jnp.where(row < wide_z, 2 * row, 2 * (row - wide_z) + 1), 1.0, 0.0
    ).astype(jnp.bfloat16)
    x_options = (((1, here),), ((2, here), (0, after)))
    for pu in range(2):
        for pv in range(2):
            left, right = [], []
            for kx, field in x_options[pu]:
                for ky, shifted in (((1, False),), ((2, False), (0, True)))[pv]:
                    left.append(taps(kx, ky))
                    right.append(down(field) if shifted else field)
            product = jnp.dot(
                jnp.concatenate(left, axis=1), jnp.concatenate(right, axis=0),
                preferred_element_type=jnp.float32,
            )
            pairs = []
            for y in range(wide_y):
                part = product[:, y * wide_z : (y + 1) * wide_z]
                even = part[cup : 2 * cup]
                odd = part[2 * cup :] + shift_down(part[:cup])
                pairs.append(jnp.concatenate([even, odd], axis=1).astype(jnp.bfloat16))
            mixed = jnp.dot(
                jnp.concatenate(pairs, axis=0), spread, preferred_element_type=jnp.float32
            ).astype(jnp.bfloat16)
            for y in range(wide_y):
                out[pu, 2 * y + pv] = mixed[y * cup : (y + 1) * cup]


def native_hidden(volume, conv_weight, bias):
    count = lax.axis_size("gx")
    forward = [(i, i + 1) for i in range(count - 1)]
    backward = [(i + 1, i) for i in range(count - 1)]
    local = lax.all_to_all(volume, "gx", split_axis=0, concat_axis=1, tiled=True)
    weight = lax.all_gather(conv_weight, "gx", axis=0, tiled=True)
    rows = local.shape[0]
    low = lax.ppermute(local[rows - 1 :], "gx", forward)
    high = lax.ppermute(local[:1], "gx", backward)
    planes = jnp.transpose(jnp.concatenate([low, local, high], axis=0), (0, 2, 1, 3))
    weight = jnp.transpose(weight, (1, 0, 2))
    cout = weight.shape[2]
    shape = jax.ShapeDtypeStruct((cout, planes.shape[1] * planes.shape[3]), jnp.bfloat16)
    conv = pl.pallas_call(
        local_conv, out_shape=shape, in_specs=[VMEM] * 3, out_specs=VMEM,
        compiler_params=pltpu.CompilerParams(vmem_limit_bytes=40 << 20),
    )
    hidden = [conv(planes[r : r + 3], weight, bias) for r in range(rows)]
    hidden.append(lax.ppermute(hidden[0], "gx", backward))
    return [jnp.stack(hidden[r : r + 2]) for r in range(rows)]


def remote_hidden(volume, conv_weight, bias):
    count = lax.axis_size("gx")
    chips = count // 2
    cells = jnp.transpose(volume, (0, 2, 1, 3))
    weight = jnp.transpose(conv_weight, (1, 0, 2))
    cout = weight.shape[2]
    lanes = cells.shape[1] * cells.shape[3]
    dma = pltpu.SemaphoreType.DMA
    hidden = pl.pallas_call(
        exchange_conv,
        out_shape=jax.ShapeDtypeStruct((2, cout, lanes), jnp.bfloat16),
        in_specs=[HBM, HBM, HBM],
        out_specs=VMEM,
        scratch_shapes=[
            pltpu.VMEM((3, count) + cells.shape[1:], jnp.bfloat16),
            pltpu.VMEM((count,) + weight.shape, jnp.bfloat16),
            pltpu.VMEM((2, cout, lanes), jnp.bfloat16),
            pltpu.VMEM((1, cout), jnp.float32),
            dma((4,)),
            dma((count,)), dma((count,)), dma((chips,)), dma((count,)),
            dma((count // 4,)), dma((count // 4,)), dma((count // 4, 2)), dma((count // 4, 2)),
            dma((chips,)), dma((chips,)), dma((2, chips)), dma((chips,)),
            dma((2, chips)), dma((2, chips)),
            dma(()), dma(()),
        ],
        compiler_params=pltpu.CompilerParams(
            collective_id=0, has_side_effects=True, vmem_limit_bytes=60 << 20
        ),
    )(cells, weight, bias.reshape(1, cout))
    return [hidden]


def per_device(volume, conv_weight, conv_bias, tconv_weight):
    count = lax.axis_size("gx")
    rows = volume.shape[0] // count
    bias = conv_bias[:, None]
    suited = (
        rows == 1 and count == 16 and lax.axis_size("groups") == 2
        and volume.shape[1] % 16 == 0
    )
    hidden = (remote_hidden if suited else native_hidden)(volume, conv_weight, bias)
    cup = tconv_weight.shape[1]
    shape = jax.ShapeDtypeStruct(
        (2, 2 * volume.shape[2], cup, 2 * volume.shape[3]), jnp.bfloat16
    )
    tconv = pl.pallas_call(
        transposed, out_shape=shape, in_specs=[VMEM] * 2, out_specs=VMEM,
        compiler_params=pltpu.CompilerParams(vmem_limit_bytes=40 << 20),
    )
    outs = [tconv(planes, tconv_weight) for planes in hidden]
    out = outs[0] if len(outs) == 1 else jnp.concatenate(outs, axis=0)
    return jnp.transpose(out, (0, 2, 1, 3))


def solution(mesh):
    return jax.shard_map(
        per_device,
        mesh=mesh,
        in_specs=(P("groups", "gx", None, None), P("gx", None, None), P(), P()),
        out_specs=P(("groups", "gx"), None, None, None),
        check_vma=False,
    )
```

```python
import jax
import jax.numpy as jnp
from jax import lax
from jax.experimental import pallas as pl
from jax.experimental.pallas import tpu as pltpu
from jax.sharding import PartitionSpec as P

MESH = pl.DeviceIdType.MESH
VMEM = pl.BlockSpec(memory_space=pltpu.VMEM)
HBM = pl.BlockSpec(memory_space=pltpu.HBM)


def shift_up(block):
    lane = lax.broadcasted_iota(jnp.int32, block.shape, 1)
    return jnp.where(lane == 0, 0.0, pltpu.roll(block, 1, axis=1))


def shift_down(block):
    size = block.shape[1]
    lane = lax.broadcasted_iota(jnp.int32, block.shape, 1)
    return jnp.where(lane == size - 1, 0.0, pltpu.roll(block, size - 1, axis=1))


def conv_hidden(planes, wide_y, wide_z, tap, bias, first=0, span=None):
    span = span or wide_y
    zero = jnp.zeros_like(planes[0](0))
    total = None
    for kx in range(3):
        padded = jnp.concatenate(
            [zero] + [planes[kx](y) for y in range(wide_y)] + [zero], axis=1
        )
        for ky in range(3):
            weight = jnp.concatenate([tap(kx * 9 + ky * 3 + kz) for kz in range(3)], axis=1)
            cells = padded[:, (ky + first) * wide_z : (ky + first + span) * wide_z]
            term = lax.dot_general(
                weight, cells, (((0,), (0,)), ((), ())), preferred_element_type=jnp.float32
            )
            total = term if total is None else total + term
    cout = total.shape[0] // 3
    rows = []
    for y in range(span):
        part = total[:, y * wide_z : (y + 1) * wide_z]
        rows.append(
            part[cout : 2 * cout]
            + shift_up(part[:cout])
            + shift_down(part[2 * cout :])
            + bias
        )
    return jnp.maximum(jnp.concatenate(rows, axis=1), 0.0).astype(jnp.bfloat16)


def exchange_conv(volume, weight, bias, hidden_out, planes, weights, hidden, bias_row, entry_sem,
                  vsend, vrecv, osend, orecv, hsend, hrecv, psend, precv,
                  wsend, rsend, wrecv, xsend, csend, crecv, esend, erecv):
    me = lax.axis_index("gx")
    count = lax.axis_size("gx")
    group = lax.axis_index("groups")
    chips = count // 2
    chip, core = me // 2, me % 2
    beds = count // 4
    bed, row = me // 4, chip % 2
    partner = me + 1 - 2 * core
    wide_y, wide_z = volume.shape[1], volume.shape[3]
    taps = weight.shape[0]
    cuts = ((0, (taps + 1) // 2), ((taps + 1) // 2, taps // 2))

    barrier = pltpu.get_barrier_semaphore()
    for d in range(1, count):
        pl.semaphore_signal(
            barrier, inc=1, device_id={"gx": (me + d) % count}, device_id_type=MESH
        )
    pl.semaphore_signal(barrier, inc=1, device_id={"groups": 1 - group}, device_id_type=MESH)
    pl.semaphore_wait(barrier, count)

    def remote(src, dst, send, recv, target):
        return pltpu.make_async_remote_copy(
            src_ref=src, dst_ref=dst, send_sem=send, recv_sem=recv,
            device_id=target, device_id_type=MESH,
        )

    def arrived(at, sem):
        pltpu.make_async_copy(at, at, sem).wait()

    inner = (me > 0) & (me < count - 1)
    outer = me - 1 + 2 * core
    own_volume = pltpu.make_async_copy(volume.at[me], planes.at[1, me], entry_sem.at[0])
    own_weight = pltpu.make_async_copy(weight, weights.at[me], entry_sem.at[1])
    own_bias = pltpu.make_async_copy(bias, bias_row, entry_sem.at[2])

    def own_outer():
        return pltpu.make_async_copy(
            volume.at[outer], planes.at[2 * core, me], entry_sem.at[3]
        )

    half = chips // 2
    place = chip % half
    base = chip - place
    mirror = (chip + half) % chips

    def near(j):
        return base + (place + j) % half

    def far(j):
        return (half - base) + (place + j) % half

    others = [mirror] + [near(j) for j in range(1, half)] + [far(j) for j in range(1, half)]

    def shard(slot, q):
        return weights.at[slot, pl.ds(*cuts[q])]

    def direct(q, j):
        to = mirror if j == 0 else near(j)
        return remote(
            weight.at[pl.ds(*cuts[q])], shard(me, q), wsend.at[j], wrecv.at[q, chip],
            {"gx": to * 2 + core},
        )

    def relay(q, j):
        at = shard(mirror * 2 + core, q)
        return remote(at, at, rsend.at[j], wrecv.at[q, mirror], {"gx": near(j) * 2 + core})

    def across(q, c):
        at = shard(c * 2 + core, q)
        return remote(at, at, xsend.at[c], wrecv.at[q, c], {"groups": 1 - group})

    def beside(q, c, own=False):
        at = shard(c * 2 + core, q)
        src = weight.at[pl.ds(*cuts[q])] if own else at
        return remote(src, at, csend.at[q, c], crecv.at[q, c], {"gx": partner})

    def piece(d):
        to = (me + d) % count
        return remote(volume.at[to], planes.at[1, me], vsend.at[d], vrecv.at[me], {"gx": to})

    def mates():
        found = [(0, partner, 1 - core)]
        for db in range(1, beds):
            for cc in range(2):
                found.append((2 * db + cc, ((bed + db) % beds) * 4 + row * 2 + cc, cc))
        return found

    def outer_piece(k, to, cc):
        return remote(
            volume.at[to - 1 + 2 * cc], planes.at[2 * cc, me], osend.at[k], orecv.at[me],
            {"gx": to},
        )

    def chunk(slot, zz, yy):
        return planes.at[slot, pl.ds(zz * 4 + yy * 2, 2)]

    def to_partner(zz, yy):
        return remote(
            chunk(1, zz, yy), chunk(2 * core, zz, yy), psend.at[zz, yy], precv.at[zz, yy],
            {"gx": partner},
        )

    def to_outer(zz):
        return remote(
            chunk(1, zz, row), chunk(2 - 2 * core, zz, row), hsend.at[zz], hrecv.at[zz],
            {"gx": outer},
        )

    order = [d for pair in zip(range(1, count // 2), range(count - 1, count // 2, -1)) for d in pair]
    order = [count // 2] + order[::-1]

    for g in range(2):
        @pl.when(group == g)
        def _(g=g):
            for j in range(half):
                direct(g, j).start()

    own_volume.start()
    @pl.when(inner)
    def _():
        own_outer().start()

    for q in range(2):
        beside(q, chip, True).start()
    own_weight.start()
    own_bias.start()

    @pl.when(me == 0)
    def _():
        planes[0] = jnp.zeros(planes.shape[1:], planes.dtype)

    @pl.when(me == count - 1)
    def _():
        planes[2] = jnp.zeros(planes.shape[1:], planes.dtype)
        hidden[1] = jnp.zeros(hidden.shape[1:], hidden.dtype)

    for g in range(2):
        @pl.when(group == g)
        def _(g=g):
            for i, c in enumerate(others):
                arrived(shard(c * 2 + core, g), wrecv.at[g, c])
                if i == 0:
                    for j in range(1, half):
                        relay(g, j).start()
                    for d in order:
                        piece(d).start()
                across(g, c).start()
                beside(g, c).start()

    for k, to, cc in mates():
        @pl.when((to > 0) & (to < count - 1))
        def _(k=k, to=to, cc=cc):
            outer_piece(k, to, cc).start()

    own_volume.wait()
    chunks = [((bed + db) % beds, yy) for yy in (row, 1 - row) for db in range(beds)]
    for i, (zz, yy) in enumerate(chunks):
        for cc in range(2):
            src = zz * 4 + yy * 2 + cc

            @pl.when(src != me)
            def _(src=src):
                arrived(planes.at[1, src], vrecv.at[src])

        to_partner(zz, yy).start()
        if i < beds:
            @pl.when(inner)
            def _(zz=zz):
                to_outer(zz).start()

    for g in range(2):
        @pl.when(group == g)
        def _(g=g):
            for c in others:
                arrived(shard(c * 2 + core, 1 - g), wrecv.at[1 - g, c])
                beside(1 - g, c).start()

    own_weight.wait()
    own_bias.wait()

    @pl.when(inner)
    def _():
        own_outer().wait()
        for k, src, cc in mates():
            arrived(planes.at[2 * core, src], orecv.at[src])
        for zz in range(beds):
            arrived(chunk(2 * core, zz, 1 - row), hrecv.at[zz])

    for zz, yy in chunks:
        arrived(chunk(2 - 2 * core, zz, yy), precv.at[zz, yy])
    for c in [chip] + others:
        for q in range(2):
            arrived(shard(c * 2 + 1 - core, q), crecv.at[q, c])

    cin = count * volume.shape[2]
    cells = [lambda y, kx=kx: planes[kx, :, y].reshape(cin, wide_z) for kx in range(3)]
    bias_cells = jnp.transpose(jnp.broadcast_to(bias_row[...], (wide_z, bias_row.shape[1])))
    span = wide_y // 2 if wide_y % 2 == 0 else wide_y
    parts = wide_y // span

    def edge(i):
        lanes = pl.ds(i * span * wide_z, span * wide_z)
        return remote(
            hidden.at[0, :, lanes], hidden.at[1, :, lanes], esend.at[i], erecv.at[i],
            {"gx": me - 1},
        )

    for i in range(parts):
        hidden[0, :, pl.ds(i * span * wide_z, span * wide_z)] = conv_hidden(
            cells, wide_y, wide_z, lambda t: weights[:, t].reshape(cin, weights.shape[3]),
            bias_cells, i * span, span,
        )

        @pl.when(me > 0)
        def _(i=i):
            edge(i).start()

    for d in order:
        piece(d).wait_send()
    for k, to, cc in mates():
        @pl.when((to > 0) & (to < count - 1))
        def _(k=k, to=to, cc=cc):
            outer_piece(k, to, cc).wait_send()

    for zz, yy in chunks:
        to_partner(zz, yy).wait_send()

    @pl.when(inner)
    def _():
        for zz in range(beds):
            to_outer(zz).wait_send()

    for g in range(2):
        @pl.when(group == g)
        def _(g=g):
            for j in range(half):
                direct(g, j).wait_send()
            for j in range(1, half):
                relay(g, j).wait_send()
            for c in others:
                across(g, c).wait_send()

    for q in range(2):
        beside(q, chip, True).wait_send()
        for c in others:
            beside(q, c).wait_send()

    @pl.when(me < count - 1)
    def _():
        for i in range(parts):
            arrived(hidden.at[1, :, pl.ds(i * span * wide_z, span * wide_z)], erecv.at[i])

    @pl.when(me > 0)
    def _():
        for i in range(parts):
            edge(i).wait_send()

    hidden_out[...] = hidden[...]


def local_conv(planes, weight, bias, hidden_out):
    wide_y, wide_z = planes.shape[1], planes.shape[3]
    cells = [lambda y, kx=kx: planes[kx, y] for kx in range(3)]
    hidden_out[...] = conv_hidden(cells, wide_y, wide_z, lambda t: weight[t], bias[...])


def transposed(hidden, tconv, out):
    wide_z = out.shape[3] // 2
    wide_y = out.shape[1] // 2
    cup = tconv.shape[1]
    cout = tconv.shape[2]
    here, after = hidden[0], hidden[1]

    def down(x):
        return jnp.concatenate([x[:, wide_z:], jnp.zeros_like(x[:, :wide_z])], axis=1)

    def taps(kx, ky):
        t = kx * 9 + ky * 3
        return tconv[t : t + 3].reshape(3 * cup, cout)

    row = lax.broadcasted_iota(jnp.int32, (2 * wide_z, 2 * wide_z), 0)
    col = lax.broadcasted_iota(jnp.int32, (2 * wide_z, 2 * wide_z), 1)
    spread = jnp.where(
        col == jnp.where(row < wide_z, 2 * row, 2 * (row - wide_z) + 1), 1.0, 0.0
    ).astype(jnp.bfloat16)
    x_options = (((1, here),), ((2, here), (0, after)))
    for pu in range(2):
        for pv in range(2):
            left, right = [], []
            for kx, field in x_options[pu]:
                for ky, shifted in (((1, False),), ((2, False), (0, True)))[pv]:
                    left.append(taps(kx, ky))
                    right.append(down(field) if shifted else field)
            product = jnp.dot(
                jnp.concatenate(left, axis=1), jnp.concatenate(right, axis=0),
                preferred_element_type=jnp.float32,
            )
            pairs = []
            for y in range(wide_y):
                part = product[:, y * wide_z : (y + 1) * wide_z]
                even = part[cup : 2 * cup]
                odd = part[2 * cup :] + shift_down(part[:cup])
                pairs.append(jnp.concatenate([even, odd], axis=1).astype(jnp.bfloat16))
            mixed = jnp.dot(
                jnp.concatenate(pairs, axis=0), spread, preferred_element_type=jnp.float32
            ).astype(jnp.bfloat16)
            for y in range(wide_y):
                out[pu, 2 * y + pv] = mixed[y * cup : (y + 1) * cup]


def native_hidden(volume, conv_weight, bias):
    count = lax.axis_size("gx")
    forward = [(i, i + 1) for i in range(count - 1)]
    backward = [(i + 1, i) for i in range(count - 1)]
    local = lax.all_to_all(volume, "gx", split_axis=0, concat_axis=1, tiled=True)
    weight = lax.all_gather(conv_weight, "gx", axis=0, tiled=True)
    rows = local.shape[0]
    low = lax.ppermute(local[rows - 1 :], "gx", forward)
    high = lax.ppermute(local[:1], "gx", backward)
    planes = jnp.transpose(jnp.concatenate([low, local, high], axis=0), (0, 2, 1, 3))
    weight = jnp.transpose(weight, (1, 0, 2))
    cout = weight.shape[2]
    shape = jax.ShapeDtypeStruct((cout, planes.shape[1] * planes.shape[3]), jnp.bfloat16)
    conv = pl.pallas_call(
        local_conv, out_shape=shape, in_specs=[VMEM] * 3, out_specs=VMEM,
        compiler_params=pltpu.CompilerParams(vmem_limit_bytes=40 << 20),
    )
    hidden = [conv(planes[r : r + 3], weight, bias) for r in range(rows)]
    hidden.append(lax.ppermute(hidden[0], "gx", backward))
    return [jnp.stack(hidden[r : r + 2]) for r in range(rows)]


def remote_hidden(volume, conv_weight, bias):
    count = lax.axis_size("gx")
    chips = count // 2
    cells = jnp.transpose(volume, (0, 2, 1, 3))
    weight = jnp.transpose(conv_weight, (1, 0, 2))
    cout = weight.shape[2]
    lanes = cells.shape[1] * cells.shape[3]
    dma = pltpu.SemaphoreType.DMA
    hidden = pl.pallas_call(
        exchange_conv,
        out_shape=jax.ShapeDtypeStruct((2, cout, lanes), jnp.bfloat16),
        in_specs=[HBM, HBM, HBM],
        out_specs=VMEM,
        scratch_shapes=[
            pltpu.VMEM((3, count) + cells.shape[1:], jnp.bfloat16),
            pltpu.VMEM((count,) + weight.shape, jnp.bfloat16),
            pltpu.VMEM((2, cout, lanes), jnp.bfloat16),
            pltpu.VMEM((1, cout), jnp.float32),
            dma((4,)),
            dma((count,)), dma((count,)), dma((chips,)), dma((count,)),
            dma((count // 4,)), dma((count // 4,)), dma((count // 4, 2)), dma((count // 4, 2)),
            dma((chips,)), dma((chips,)), dma((2, chips)), dma((chips,)),
            dma((2, chips)), dma((2, chips)),
            dma((2,)), dma((2,)),
        ],
        compiler_params=pltpu.CompilerParams(
            collective_id=0, has_side_effects=True, vmem_limit_bytes=60 << 20
        ),
    )(cells, weight, bias.reshape(1, cout))
    return [hidden]


def per_device(volume, conv_weight, conv_bias, tconv_weight):
    count = lax.axis_size("gx")
    rows = volume.shape[0] // count
    bias = conv_bias[:, None]
    suited = (
        rows == 1 and count == 16 and lax.axis_size("groups") == 2
        and volume.shape[1] % 16 == 0
    )
    hidden = (remote_hidden if suited else native_hidden)(volume, conv_weight, bias)
    cup = tconv_weight.shape[1]
    shape = jax.ShapeDtypeStruct(
        (2, 2 * volume.shape[2], cup, 2 * volume.shape[3]), jnp.bfloat16
    )
    tconv = pl.pallas_call(
        transposed, out_shape=shape, in_specs=[VMEM] * 2, out_specs=VMEM,
        compiler_params=pltpu.CompilerParams(vmem_limit_bytes=40 << 20),
    )
    outs = [tconv(planes, tconv_weight) for planes in hidden]
    out = outs[0] if len(outs) == 1 else jnp.concatenate(outs, axis=0)
    return jnp.transpose(out, (0, 2, 1, 3))


def solution(mesh):
    return jax.shard_map(
        per_device,
        mesh=mesh,
        in_specs=(P("groups", "gx", None, None), P("gx", None, None), P(), P()),
        out_specs=P(("groups", "gx"), None, None, None),
        check_vma=False,
    )
```
